512 devices in a mesh: seq: 32 (over y, x), head: 16 (over z, core).
Axes of the slice: x: 4, y: 8, z: 8, core: 2. Of those that a mesh axis runs over, the one named last changes fastest.
Arguments:
- queries: bfloat16 [65536, 2048], P('seq', 'head'), may hold values from -4.5 to 4.5
- key_vectors: bfloat16 [65536, 2048], P('seq', 'head'), may hold values from -4.5 to 4.5
- value_vectors: bfloat16 [65536, 2048], P('seq', 'head'), may hold values from -18 to 18
- w_out: bfloat16 [2048, 2048], P('seq'), may hold values from -0.125 to 0.125
Outputs:
- projected: bfloat16 [65536, 2048], P(('seq', 'head'))
The draws below stay inside these ranges and needn't reach their ends.
All inputs are finite; a program needn't handle non-finite values.
Results may differ from the reference program's by a relative error of at most 0.0053.
Values may be sent and summed in bfloat16 or wider, within the bound.
No kernel may reach another device: no remote copies, remote signals or barrier semaphores. Data moves between devices by JAX's collectives and lax.ppermute only.
A program may use at most 64 MiB of HBM per device.

```python
import math
import jax
import jax.numpy as jnp
from jax import lax

H = 16
HD = 128
W = 1024
D = 2048
TOKENS = 65536


def draw_queries(key, part):
    base_key = jax.random.fold_in(key, 1)
    base_draw = jax.random.truncated_normal(base_key, -4.5, 4.5, (TOKENS, D), jnp.float32)
    return base_draw.astype(jnp.bfloat16)


def draw_key_vectors(key, part):
    base_key = jax.random.fold_in(key, 2)
    base_draw = jax.random.truncated_normal(base_key, -4.5, 4.5, (TOKENS, D), jnp.float32)
    return base_draw.astype(jnp.bfloat16)


def draw_value_vectors(key, part):
    row_scale = jnp.exp(jax.random.uniform(jax.random.fold_in(key, 1), (TOKENS, 1), jnp.float32, math.log(0.3), math.log(3.0)))
    col_scale = jnp.exp(jax.random.uniform(jax.random.fold_in(key, 2), (1, D), jnp.float32, math.log(0.5), math.log(2.0)))
    noise_draw = jax.random.truncated_normal(jax.random.fold_in(key, 4), -3.0, 3.0, (TOKENS, D), jnp.float32)
    drawn = row_scale * col_scale * noise_draw
    return drawn.astype(jnp.bfloat16)


def shard_levels(own_key, extent, pieces, least, largest):
    def one(dim, shards_of):
        draws = jax.random.uniform(jax.random.fold_in(jax.random.fold_in(own_key, 6), dim), (shards_of,), jnp.float32, least / len(pieces), largest / len(pieces))
        return jnp.repeat(jnp.exp(draws), extent[dim] // shards_of).reshape((-1,) + (1,) * (len(extent) - dim - 1))

    factor_of = one(*pieces[0])
    for cut in pieces[1:]:
        factor_of = factor_of * one(*cut)
    return factor_of


def normal_values(rng, shape, width, bound, cuts=(), kind=jnp.bfloat16):
    factor_of = shard_levels(rng, shape, cuts, -0.22, 0.18) if cuts else 1.0
    array = jax.random.normal(rng, shape, jnp.float32) * width * factor_of
    return jnp.minimum(jnp.maximum(array, -bound), bound).astype(kind)


def setup_inputs(seed: int = 0) -> dict:
    key_of = jax.random.split(jax.random.key(seed), 5)
    return {
        "queries": draw_queries(jax.random.fold_in(key_of[4], 71), 0),
        "key_vectors": draw_key_vectors(jax.random.fold_in(key_of[4], 71), 0),
        "value_vectors": draw_value_vectors(jax.random.fold_in(key_of[4], 71), 0),
        "w_out": normal_values(key_of[3], (D, D), D ** -0.5, 0.125, ((0, 32),)),
    }


norm_eps = 1e-06

def normalize(branch):
    return branch * lax.rsqrt(lax.optimization_barrier(jnp.mean(branch * branch, axis=-1, keepdims=True)) + norm_eps)

def window_head(query_head, key_head, value_head):
    block_rows = math.gcd(TOKENS, 256)
    key_span = block_rows + W
    score_scale = 1.0 / math.sqrt(HD)
    window_keys = jnp.concatenate([jnp.zeros((W, HD), jnp.bfloat16), key_head], axis=0)
    window_values = jnp.concatenate([jnp.zeros((W, HD), jnp.bfloat16), value_head], axis=0)

    def one_block(block_start):
        query_block = lax.dynamic_slice_in_dim(query_head, block_start, block_rows, 0)
        key_block = lax.dynamic_slice_in_dim(window_keys, block_start, key_span, 0)
        value_block = lax.dynamic_slice_in_dim(window_values, block_start, key_span, 0)
        scores = jnp.dot(query_block, key_block.T, preferred_element_type=jnp.float32) * score_scale
        row_index = block_start + jnp.arange(block_rows, dtype=jnp.int32)[:, None]
        col_index = block_start + jnp.arange(key_span, dtype=jnp.int32)[None, :]
        allowed = (col_index > row_index) & (col_index <= row_index + W) & (col_index >= W)
        scores = jnp.where(allowed, scores, -jnp.inf)
        row_top = lax.optimization_barrier(jnp.max(scores, axis=-1, keepdims=True))
        weights = jnp.where(allowed, jnp.exp(scores - row_top), 0.0).astype(jnp.bfloat16)
        return jnp.dot(weights, value_block, preferred_element_type=jnp.float32)
    starts = jnp.arange(TOKENS // block_rows, dtype=jnp.int32) * block_rows
    return lax.map(one_block, starts).reshape(TOKENS, HD)

def linear_head(query_head, key_head, value_head):
    block_rows = math.gcd(TOKENS, 512)
    block_count = TOKENS // block_rows
    exact_output = lax.Precision.HIGHEST
    blocked_queries = query_head.reshape(block_count, block_rows, HD).astype(jnp.float32)
    blocked_keys = key_head.reshape(block_count, block_rows, HD).astype(jnp.float32)
    blocked_values = value_head.reshape(block_count, block_rows, HD).astype(jnp.float32)
    intra_block_scores = jnp.einsum('upn,uwn->upw', blocked_queries, blocked_keys, precision=exact_output)
    causal = jnp.arange(block_rows, dtype=jnp.int32)[:, None] >= jnp.arange(block_rows, dtype=jnp.int32)[None, :]
    intra_block_scores = jnp.where(causal[None], intra_block_scores, 0.0)
    local_block_terms = jnp.einsum('vyc,vca->vya', intra_block_scores, blocked_values, precision=exact_output)
    state_increments = jnp.einsum('tsp,tsw->tpw', blocked_keys, blocked_values, precision=exact_output)
    running = jnp.cumsum(state_increments, axis=0)
    preceding_state = jnp.concatenate([jnp.zeros_like(state_increments[:1]), running[:-1]], axis=0)
    carried_state_sum = jnp.einsum('viu,vuh->vih', blocked_queries, preceding_state, precision=exact_output)
    return (local_block_terms + carried_state_sum).reshape(TOKENS, HD)

def reference(queries, key_vectors, value_vectors, w_out):
    head_shape = (TOKENS, H, HD)
    query_heads = jnp.transpose(queries.reshape(head_shape), (1, 0, 2))
    key_heads = jnp.transpose(key_vectors.reshape(head_shape), (1, 0, 2))
    value_heads = jnp.transpose(value_vectors.reshape(head_shape), (1, 0, 2))

    def per_head(triple):
        query_head, key_head, value_head = triple
        soft_head = window_head(query_head, key_head, value_head)
        linear = linear_head(query_head, key_head, value_head)
        return (0.5 * (normalize(soft_head) + normalize(linear))).astype(jnp.bfloat16)
    mixed_heads = lax.map(per_head, (query_heads, key_heads, value_heads))
    attended = jnp.transpose(mixed_heads, (1, 0, 2)).reshape(TOKENS, D)
    return jnp.dot(attended, w_out, preferred_element_type=jnp.float32).astype(jnp.bfloat16)
```

```python
import functools
import math

import jax
import jax.numpy as jnp
from jax import lax
from jax.experimental import pallas as pl
from jax.experimental.pallas import tpu as pltpu
from jax.sharding import Mesh
from jax.sharding import PartitionSpec as P

HD = 128
W = 1024
BLOCK = 256
NY, NX, NZ, NC = 8, 4, 8, 2
AXES = ("y", "x", "z", "c")

norm_eps = 1e-06
log2e_scale = math.log2(math.e) / math.sqrt(HD)
far_below = -1e30

f32, bf16 = jnp.float32, jnp.bfloat16


def dot(a, b):
    return lax.dot_general(a, b, (((1,), (0,)), ((), ())), preferred_element_type=f32)


def dot_nt(a, b):
    return lax.dot_general(a, b, (((1,), (1,)), ((), ())), preferred_element_type=f32)


def dot_tn(a, b):
    return lax.dot_general(a, b, (((0,), (0,)), ((), ())), preferred_element_type=f32)


def normalize(branch):
    return branch * lax.rsqrt(jnp.mean(branch * branch, axis=-1, keepdims=True) + norm_eps)


def split_pair(values):
    upper = values.astype(bf16)
    return upper, (values - upper.astype(f32)).astype(bf16)


VMEM = pl.BlockSpec(memory_space=pltpu.VMEM)
SMEM = pl.BlockSpec(memory_space=pltpu.SMEM)


def call(kernel, name, outs, in_specs, flops, trans=0, nbytes=1 << 20, scratch=()):
    return pl.pallas_call(
        kernel,
        name=name,
        out_shape=outs,
        in_specs=in_specs,
        out_specs=jax.tree.map(lambda _: VMEM, outs),
        scratch_shapes=scratch,
        cost_estimate=pl.CostEstimate(flops=flops, transcendentals=trans, bytes_accessed=nbytes),
    )


def state_kernel(k_ref, v_ref, out_ref):
    total = dot_tn(k_ref[...], v_ref[...])
    for i in range(NX):
        out_ref[i] = total


def row_kernel(place_ref, states_ref, before_ref, total_ref):
    x = place_ref[1]
    before = jnp.zeros((HD, HD), f32)
    total = jnp.zeros((HD, HD), f32)
    for i in range(NX):
        state = states_ref[i]
        total = total + state
        before = before + jnp.where(i < x, state, 0.0)
    before_ref[...] = before
    sent = total.astype(bf16)
    for i in range(NY):
        total_ref[i] = sent


def window_rows(q, keys, values, bias, upper):
    key_blocks = [dot_nt(q, key) for key in keys]
    if bias is not None:
        key_blocks = [s + b if b is not None else s for s, b in zip(key_blocks, bias)]
    ends = jnp.where(upper, key_blocks[0], key_blocks[-1])
    scores = [ends] + key_blocks[1:-1]
    top = scores[0]
    for s in scores[1:]:
        top = jnp.maximum(top, s)
    top = jnp.max(top, axis=-1, keepdims=True)
    weights = [jnp.exp2((s - top) * log2e_scale) for s in scores]
    ends = weights[0]
    parts = [jnp.where(upper, ends, 0.0)] + weights[1:] + [jnp.where(upper, 0.0, ends)]
    soft = None
    for part, value in zip(parts, values):
        term = dot(part.astype(bf16), value)
        soft = term if soft is None else soft + term
    return normalize(soft) * 0.5


def upper_mask():
    rows = lax.broadcasted_iota(jnp.int32, (BLOCK, BLOCK), 0)
    cols = lax.broadcasted_iota(jnp.int32, (BLOCK, BLOCK), 1)
    return cols > rows


def rows_of(ref, index):
    return ref[index * BLOCK : (index + 1) * BLOCK, :]


def inner_kernel(q_ref, k_ref, v_ref, out_ref):
    upper = upper_mask()
    near = W // BLOCK
    for b in range(near):
        keys = [rows_of(k_ref, b + j) for j in range(near + 1)]
        values = [rows_of(v_ref, b + j) for j in range(near + 1)]
        out_ref[b * BLOCK : (b + 1) * BLOCK, :] = window_rows(
            rows_of(q_ref, near + b), keys, values, None, upper
        )


def outer_kernel(place_ref, q_ref, k_ref, v_ref, rim_ref, out_ref):
    upper = upper_mask()
    near = W // BLOCK
    first = jnp.logical_and(place_ref[0] == 0, place_ref[1] == 0)
    hidden = jnp.where(first, far_below, 0.0).astype(f32)
    for b in range(near):
        keys, values, bias = [], [], []
        for j in range(near + 1):
            at = b + j
            if at < near:
                keys.append(rim_ref[0, at * BLOCK : (at + 1) * BLOCK, :])
                values.append(rim_ref[1, at * BLOCK : (at + 1) * BLOCK, :])
                bias.append(hidden)
            else:
                keys.append(rows_of(k_ref, at - near))
                values.append(rows_of(v_ref, at - near))
                bias.append(None)
        out_ref[b * BLOCK : (b + 1) * BLOCK, :] = window_rows(
            rows_of(q_ref, b), keys, values, bias, upper
        )


def local_kernel(q_ref, k_ref, v_ref, out_ref):
    causal = jnp.logical_not(upper_mask())
    state = None
    for b in range(q_ref.shape[0] // BLOCK):
        q, k, v = rows_of(q_ref, b), rows_of(k_ref, b), rows_of(v_ref, b)
        upper, lower = split_pair(jnp.where(causal, dot_nt(q, k), 0.0))
        linear = dot(upper, v) + dot(lower, v)
        if state is not None:
            upper, lower = split_pair(state)
            both = dot(q, jnp.concatenate([upper, lower], axis=1))
            linear = linear + (both[:, :HD] + both[:, HD:])
        out_ref[b * BLOCK : (b + 1) * BLOCK, :] = linear
        own = dot_tn(k, v)
        state = own if state is None else state + own


def mix_kernel(place_ref, q_ref, linear_ref, outer_ref, inner_ref, before_ref, totals_ref, out_ref):
    y = place_ref[0]
    state = before_ref[...]
    for i in range(NY):
        state = state + jnp.where(i < y, totals_ref[i].astype(f32), 0.0)
    upper, lower = split_pair(state)
    state = jnp.concatenate([upper, lower], axis=1)
    half = W // BLOCK
    for b in range(q_ref.shape[0] // BLOCK):
        both = dot(rows_of(q_ref, b), state)
        linear = rows_of(linear_ref, b) + (both[:, :HD] + both[:, HD:])
        soft = rows_of(outer_ref, b) if b < half else rows_of(inner_ref, b - half)
        out_ref[b] = (soft + normalize(linear) * 0.5).astype(bf16)


def project_kernel(take_ref, mixed_ref, *refs):
    units, out_ref = refs[:-1], refs[-1]
    start = pl.multiple_of(take_ref[0] * HD, HD)
    parts = [mixed_ref[take_ref[1 + i], pl.ds(start, HD), :] for i in range(NY)]
    width = 512
    for n in range(out_ref.shape[1] // width):
        cols = slice(n * width, (n + 1) * width)
        total = None
        for i in range(0, NY, 2):
            pair = jnp.concatenate([parts[i], parts[i + 1]], axis=1)
            rows = jnp.concatenate([units[i][:, cols], units[i + 1][:, cols]], axis=0)
            term = dot(pair, rows)
            total = term if total is None else total + term
        out_ref[:, cols] = total.astype(out_ref.dtype)


def linear_index(y, x, z, c):
    return ((y % NY * NX + x % NX) * NZ + z % NZ) * NC + c


def moved(shard, source):
    pairs = []
    for y in range(NY):
        for x in range(NX):
            for z in range(NZ):
                for c in range(NC):
                    at = source(y, x, z, c)
                    if at is not None:
                        pairs.append((linear_index(*at), linear_index(y, x, z, c)))
    return lax.ppermute(shard, AXES, pairs)


def first_chunk(y, x, z, c):
    if x // 2 == c:
        return (y, x ^ 1, z, 1 - c)
    return (y, 3 - x, z, c)


def second_chunk(y, x, z, c):
    return None if x // 2 == c else (y, x ^ 2, z, c)


def way(z, c):
    return 1 - 2 * ((z + c) % 2)


def along(y, x, z, c):
    return (y + way(z, c), x, z, c)


def across(y, x, z, c):
    return (y, x, (z ^ 1) if c == 0 else ((z + 1) ^ 1) - 1, c)


def on_device(queries, key_vectors, value_vectors, w_out):
    y, x, z, c = (lax.axis_index(a) for a in AXES)
    place = jnp.stack([y, x, z, c]).astype(jnp.int32)
    rows = queries.shape[0]
    wide = w_out.shape[1]

    chunk_a = moved(w_out, first_chunk)
    chunk_b = moved(w_out, second_chunk)

    states = call(
        state_kernel, "state", jax.ShapeDtypeStruct((NX, HD, HD), f32), [VMEM, VMEM],
        2 * rows * HD * HD,
    )(key_vectors, value_vectors)
    row_states = lax.all_to_all(states, "x", 0, 0, tiled=True)

    rim = jnp.stack([key_vectors[rows - W :], value_vectors[rows - W :]])
    rim = lax.ppermute(rim, ("y", "x"), [(i, i + 1) for i in range(NY * NX - 1)])

    own = jnp.where(x // 2 == c, w_out, chunk_b)
    even = x % 2 == 0
    unit = jnp.concatenate([jnp.where(even, own, chunk_a), jnp.where(even, chunk_a, own)], axis=0)
    y1 = moved(unit, along)
    z1 = moved(y1, across)
    y2 = moved(y1, along)
    z2 = moved(y2, across)
    y3 = moved(y2, along)
    z3 = moved(y3, across)
    y4 = moved(y3, along)

    before, totals = call(
        row_kernel, "row",
        (jax.ShapeDtypeStruct((HD, HD), f32), jax.ShapeDtypeStruct((NY, HD, HD), bf16)),
        [SMEM, VMEM], 8 * HD * HD,
    )(place, row_states)
    totals = lax.all_to_all(totals, "y", 0, 0, tiled=True)

    half = jax.ShapeDtypeStruct((W, HD), f32)
    work = 2 * W * (W + BLOCK) * HD * 2
    inner = call(inner_kernel, "inner", half, [VMEM] * 3, work, W * W)(
        queries, key_vectors, value_vectors
    )
    linear = call(
        local_kernel, "local", jax.ShapeDtypeStruct((rows, HD), f32), [VMEM] * 3,
        2 * rows * BLOCK * HD * 4,
    )(queries, key_vectors, value_vectors)
    outer = call(outer_kernel, "outer", half, [SMEM] + [VMEM] * 4, work, W * W)(
        place, queries, key_vectors, value_vectors, rim
    )
    mixed = call(
        mix_kernel, "mix", jax.ShapeDtypeStruct((NZ, rows // NZ, HD), bf16), [SMEM] + [VMEM] * 6,
        4 * rows * HD * HD,
    )(place, queries, linear, outer, inner, before, totals)
    mixed = lax.all_to_all(mixed, "z", 0, 0, tiled=True)

    turn = way(z, c)
    units = (unit, y1, y2, y3, y4, z1, z2, z3)
    steps = (0, 1, 2, 3, 4, -1, -2, -3)
    at = [(y + turn * s) % NY for s in steps]

    def project(share, dtype):
        take = jnp.stack([share] + at).astype(jnp.int32)
        return call(
            project_kernel, "project", jax.ShapeDtypeStruct((HD, wide), dtype),
            [SMEM] + [VMEM] * (1 + NY), 2 * HD * wide * NY * HD, 0, NY * HD * wide * 2,
        )(take, mixed, *units)

    given = project(1 - c, bf16)
    taken = lax.ppermute(given, "c", [(0, 1), (1, 0)])
    kept = project(c, f32)
    return (kept + taken.astype(f32)).astype(bf16)


def solution(mesh):
    fine = Mesh(mesh.devices.reshape(NY, NX, NZ, NC), AXES)
    split = P(("y", "x"), ("z", "c"))
    return jax.shard_map(
        on_device,
        mesh=fine,
        in_specs=(split, split, split, P(("y", "x"), None)),
        out_specs=P(AXES, None),
        check_vma=False,
    )
```

```python
import math

import jax
import jax.numpy as jnp
from jax import lax
from jax.experimental import pallas as pl
from jax.experimental.pallas import tpu as pltpu
from jax.sharding import Mesh
from jax.sharding import PartitionSpec as P

HD = 128
W = 1024
BLOCK = 256
NY, NX, NZ, NC = 8, 4, 8, 2
AXES = ("y", "x", "z", "c")

norm_eps = 1e-06
log2e_scale = math.log2(math.e) / math.sqrt(HD)
far_below = -1e30

f32, bf16 = jnp.float32, jnp.bfloat16


def dot(a, b):
    return lax.dot_general(a, b, (((1,), (0,)), ((), ())), preferred_element_type=f32)


def dot_nt(a, b):
    return lax.dot_general(a, b, (((1,), (1,)), ((), ())), preferred_element_type=f32)


def dot_tn(a, b):
    return lax.dot_general(a, b, (((0,), (0,)), ((), ())), preferred_element_type=f32)


def normalize(branch):
    return branch * lax.rsqrt(jnp.mean(branch * branch, axis=-1, keepdims=True) + norm_eps)


def split_pair(values):
    upper = values.astype(bf16)
    return upper, (values - upper.astype(f32)).astype(bf16)


VMEM = pl.BlockSpec(memory_space=pltpu.VMEM)
SMEM = pl.BlockSpec(memory_space=pltpu.SMEM)


def call(kernel, outs, in_specs, flops, trans=0, nbytes=1 << 20):
    return pl.pallas_call(
        kernel,
        out_shape=outs,
        in_specs=in_specs,
        out_specs=jax.tree.map(lambda _: VMEM, outs),
        compiler_params=pltpu.CompilerParams(vmem_limit_bytes=12 << 20),
        cost_estimate=pl.CostEstimate(flops=flops, transcendentals=trans, bytes_accessed=nbytes),
    )


def rows_of(ref, index):
    return ref[index * BLOCK : (index + 1) * BLOCK, :]


def state_kernel(k_ref, v_ref, out_ref, before_ref, rim_ref):
    count = k_ref.shape[0] // BLOCK
    total = jnp.zeros((HD, HD), f32)
    for b in range(count):
        before_ref[b] = total
        total = total + dot_tn(rows_of(k_ref, b), rows_of(v_ref, b))
    for i in range(NX):
        out_ref[i] = total
    rim_ref[0] = k_ref[k_ref.shape[0] - W :, :]
    rim_ref[1] = v_ref[v_ref.shape[0] - W :, :]


def row_kernel(states_ref, before_ref, total_ref):
    x = lax.axis_index("x")
    before = jnp.zeros((HD, HD), f32)
    total = jnp.zeros((HD, HD), f32)
    for i in range(NX):
        state = states_ref[i]
        total = total + state
        before = before + jnp.where(i < x, state, 0.0)
    before_ref[...] = before
    sent = total.astype(bf16)
    for i in range(NY):
        total_ref[i] = sent


def block_rows(q, keys, values, bias, upper):
    key_blocks = [dot_nt(q, key) for key in keys]
    near = key_blocks[-1]
    high, low = split_pair(jnp.where(upper, 0.0, near))
    linear = dot(high, values[-1]) + dot(low, values[-1])
    if bias is not None:
        key_blocks = [s if b is None else s + b for s, b in zip(key_blocks, bias)]
    scores = [jnp.where(upper, key_blocks[0], near)] + key_blocks[1:-1]
    top = scores[0]
    for s in scores[1:]:
        top = jnp.maximum(top, s)
    top = jnp.max(top, axis=-1, keepdims=True)
    weights = [jnp.exp2((s - top) * log2e_scale) for s in scores]
    ends = weights[0]
    parts = [jnp.where(upper, ends, 0.0)] + weights[1:] + [jnp.where(upper, 0.0, ends)]
    soft = None
    for part, value in zip(parts, values):
        term = dot(part.astype(bf16), value)
        soft = term if soft is None else soft + term
    return normalize(soft) * 0.5, linear


def upper_mask():
    rows = lax.broadcasted_iota(jnp.int32, (BLOCK, BLOCK), 0)
    cols = lax.broadcasted_iota(jnp.int32, (BLOCK, BLOCK), 1)
    return cols > rows


def inner_kernel(q_ref, k_ref, v_ref, soft_ref, linear_ref):
    upper = upper_mask()
    near = W // BLOCK
    for b in range(near):
        keys = [rows_of(k_ref, b + j) for j in range(near + 1)]
        values = [rows_of(v_ref, b + j) for j in range(near + 1)]
        soft, linear = block_rows(rows_of(q_ref, near + b), keys, values, None, upper)
        soft_ref[b * BLOCK : (b + 1) * BLOCK, :] = soft
        linear_ref[b * BLOCK : (b + 1) * BLOCK, :] = linear


def outer_kernel(q_ref, k_ref, v_ref, rim_ref, soft_ref, linear_ref):
    upper = upper_mask()
    near = W // BLOCK
    first = jnp.logical_and(lax.axis_index("y") == 0, lax.axis_index("x") == 0)
    hidden = jnp.where(first, far_below, 0.0).astype(f32)
    for b in range(near):
        keys, values, bias = [], [], []
        for j in range(near + 1):
            at = b + j
            if at < near:
                keys.append(rim_ref[0, at * BLOCK : (at + 1) * BLOCK, :])
                values.append(rim_ref[1, at * BLOCK : (at + 1) * BLOCK, :])
                bias.append(hidden)
            else:
                keys.append(rows_of(k_ref, at - near))
                values.append(rows_of(v_ref, at - near))
                bias.append(None)
        soft, linear = block_rows(rows_of(q_ref, b), keys, values, bias, upper)
        soft_ref[b * BLOCK : (b + 1) * BLOCK, :] = soft
        linear_ref[b * BLOCK : (b + 1) * BLOCK, :] = linear


def mix_kernel(
    q_ref, outer_ref, outer_linear_ref, inner_ref, inner_linear_ref, within_ref, before_ref, totals_ref, out_ref
):
    y = lax.axis_index("y")
    odd = lax.axis_index("x") % 2 == 1
    shift = jnp.where(odd, HD // 2, 0)
    prior = before_ref[...]
    for i in range(NY):
        prior = prior + jnp.where(i < y, totals_ref[i].astype(f32), 0.0)
    half = W // BLOCK
    for b in range(q_ref.shape[0] // BLOCK):
        upper, lower = split_pair(prior + within_ref[b])
        both = dot(rows_of(q_ref, b), jnp.concatenate([upper, lower], axis=1))
        near = rows_of(outer_linear_ref, b) if b < half else rows_of(inner_linear_ref, b - half)
        soft = rows_of(outer_ref, b) if b < half else rows_of(inner_ref, b - half)
        linear = near + (both[:, :HD] + both[:, HD:])
        mixed = soft + normalize(linear) * 0.5
        out_ref[b] = pltpu.roll(mixed, shift, 1).astype(bf16)


def project_kernel(mixed_ref, *refs):
    units, given_ref, kept_ref = refs[:-2], refs[-2], refs[-1]
    y, z, c = lax.axis_index("y"), lax.axis_index("z"), lax.axis_index("c")
    turn = way(z, c)
    given, kept = [], []
    for step in unit_steps:
        head = lax.rem(y + turn * step + NY, NY)
        given.append(mixed_ref[head, pl.ds(pl.multiple_of((1 - c) * HD, HD), HD), :])
        kept.append(mixed_ref[head, pl.ds(pl.multiple_of(c * HD, HD), HD), :])
    left = [
        jnp.concatenate(
            [jnp.concatenate(given[i : i + 2], axis=1), jnp.concatenate(kept[i : i + 2], axis=1)], axis=0
        )
        for i in range(0, NY, 2)
    ]
    width = 512
    for n in range(kept_ref.shape[1] // width):
        cols = slice(n * width, (n + 1) * width)
        total = None
        for i in range(0, NY, 2):
            rows = jnp.concatenate([units[i][:, cols], units[i + 1][:, cols]], axis=0)
            term = dot(left[i // 2], rows)
            total = term if total is None else total + term
        given_ref[:, cols] = total[:HD].astype(bf16)
        kept_ref[:, cols] = total[HD:]


def add_kernel(kept_ref, taken_ref, out_ref):
    out_ref[...] = (kept_ref[...] + taken_ref[...].astype(f32)).astype(bf16)


def linear_index(y, x, z, c):
    return ((y % NY * NX + x % NX) * NZ + z % NZ) * NC + c


def moved(shard, source):
    pairs = []
    for y in range(NY):
        for x in range(NX):
            for z in range(NZ):
                for c in range(NC):
                    at = source(y, x, z, c)
                    if at is not None:
                        pairs.append((linear_index(*at), linear_index(y, x, z, c)))
    return lax.ppermute(shard, AXES, pairs)


def first_chunk(y, x, z, c):
    if x // 2 == c:
        return (y, x ^ 1, z, 1 - c)
    return (y, 3 - x, z, c)


def second_chunk(y, x, z, c):
    return (y, x, z, 1 - c) if x // 2 == c else (y, x ^ 2, z, c)


unit_steps = (0, 1, 2, 3, 4, -1, -2, -3)


def way(z, c):
    return 1 - 2 * ((z + c) % 2)


def along(y, x, z, c):
    return (y + way(z, c), x, z, c)


def across(y, x, z, c):
    return (y, x, (z ^ 1) if c == 0 else ((z + 1) ^ 1) - 1, c)


def layer(queries, key_vectors, value_vectors, w_out):
    rows = queries.shape[0]
    wide = w_out.shape[1]

    def shape(dims, kind):
        return jax.ShapeDtypeStruct(dims, kind)

    chunk_a = moved(w_out, first_chunk)
    chunk_b = moved(w_out, second_chunk)
    states, within, rim = call(
        state_kernel,
        (shape((NX, HD, HD), f32), shape((rows // BLOCK, HD, HD), f32), shape((2, W, HD), bf16)),
        [VMEM] * 2, 2 * rows * HD * HD,
    )(key_vectors, value_vectors)
    row_states = lax.all_to_all(states, "x", 0, 0, tiled=True)
    unit = jnp.concatenate([chunk_b, chunk_a], axis=0)
    y1 = moved(unit, along)
    rim = lax.ppermute(rim, ("y", "x"), [(i, i + 1) for i in range(NY * NX - 1)])
    before, totals = call(
        row_kernel, (shape((HD, HD), f32), shape((NY, HD, HD), bf16)), [VMEM], 8 * HD * HD
    )(row_states)
    totals = lax.all_to_all(totals, "y", 0, 0, tiled=True)
    y2 = moved(y1, along)
    z1 = moved(y1, across)
    half = shape((W, HD), f32)
    work = 2 * W * (W + BLOCK) * HD * 2
    inner, inner_linear = call(inner_kernel, (half, half), [VMEM] * 3, work, W * W)(
        queries, key_vectors, value_vectors
    )
    y3 = moved(y2, along)
    z2 = moved(y2, across)
    outer, outer_linear = call(outer_kernel, (half, half), [VMEM] * 4, work, W * W)(
        queries, key_vectors, value_vectors, rim
    )
    y4 = moved(y3, along)
    z3 = moved(y3, across)
    mixed = call(
        mix_kernel, shape((NZ, rows // NZ, HD), bf16), [VMEM] * 8, 4 * rows * HD * HD
    )(queries, outer, outer_linear, inner, inner_linear, within, before, totals)
    mixed = lax.all_to_all(mixed, "z", 0, 0, tiled=True)
    given, kept = call(
        project_kernel, (shape((HD, wide), bf16), shape((HD, wide), f32)),
        [VMEM] * (1 + NY), 4 * HD * wide * NY * HD, 0, NY * HD * wide * 2,
    )(mixed, unit, y1, y2, y3, y4, z1, z2, z3)
    taken = lax.ppermute(given, "c", [(0, 1), (1, 0)])
    return call(add_kernel, shape((HD, wide), bf16), [VMEM] * 2, HD * wide)(kept, taken)


def solution(mesh):
    fine = Mesh(mesh.devices.reshape(NY, NX, NZ, NC), AXES)
    split = P(("y", "x"), ("z", "c"))
    return jax.shard_map(
        layer,
        mesh=fine,
        in_specs=(split, split, split, P(("y", "x"), None)),
        out_specs=P(AXES, None),
        check_vma=False,
    )
```

```python
import math

import jax
import jax.numpy as jnp
from jax import lax
from jax.experimental import pallas as pl
from jax.experimental.pallas import tpu as pltpu
from jax.sharding import Mesh
from jax.sharding import PartitionSpec as P

HD = 128
W = 1024
BLOCK = 256
FETCHES = 4
NY, NX, NZ, NC = 8, 4, 8, 2
AXES = ("y", "x", "z", "c")

norm_eps = 1e-06
log2e_scale = math.log2(math.e) / math.sqrt(HD)
far_below = -1e30

f32, bf16 = jnp.float32, jnp.bfloat16


def dot(a, b):
    return lax.dot_general(a, b, (((1,), (0,)), ((), ())), preferred_element_type=f32)


def dot_nt(a, b):
    return lax.dot_general(a, b, (((1,), (1,)), ((), ())), preferred_element_type=f32)


def dot_tn(a, b):
    return lax.dot_general(a, b, (((0,), (0,)), ((), ())), preferred_element_type=f32)


def normalize(branch):
    return branch * lax.rsqrt(jnp.mean(branch * branch, axis=-1, keepdims=True) + norm_eps)


def split_pair(values):
    upper = values.astype(bf16)
    return upper, (values - upper.astype(f32)).astype(bf16)


VMEM = pl.BlockSpec(memory_space=pltpu.VMEM)
ANY = pl.BlockSpec(memory_space=pl.ANY)


def call(kernel, outs, in_specs, scratch=(), grant=12 << 20, out_specs=None):
    return pl.pallas_call(
        kernel,
        out_shape=outs,
        in_specs=in_specs,
        scratch_shapes=scratch,
        out_specs=out_specs or jax.tree.map(lambda _: VMEM, outs),
        compiler_params=pltpu.CompilerParams(vmem_limit_bytes=grant),
        cost_estimate=pl.CostEstimate(flops=1, transcendentals=0, bytes_accessed=64 << 20),
    )


def rows_of(ref, index):
    return ref[index * BLOCK : (index + 1) * BLOCK, :]


def state_kernel(k_hbm, v_hbm, out_hbm, before_hbm, rim_hbm, k_ref, v_ref, before_ref, total_ref, sems, out_sems):
    chunk = k_hbm.shape[0] // FETCHES
    copies = []
    for i in range(FETCHES):
        part = pl.ds(i * chunk, chunk)
        pair = (
            pltpu.make_async_copy(k_hbm.at[part], k_ref.at[part], sems.at[0, i]),
            pltpu.make_async_copy(v_hbm.at[part], v_ref.at[part], sems.at[1, i]),
        )
        for copy in pair:
            copy.start()
        copies.append(pair)
    tail = pl.ds(k_hbm.shape[0] - W, W)
    sent = [
        pltpu.make_async_copy(k_ref.at[tail], rim_hbm.at[0], out_sems.at[0]),
        pltpu.make_async_copy(v_ref.at[tail], rim_hbm.at[1], out_sems.at[1]),
    ]
    total = jnp.zeros((HD, HD), f32)
    for i in range(FETCHES):
        for copy in copies[i]:
            copy.wait()
        if i == FETCHES - 1:
            for copy in sent:
                copy.start()
        for b in range(i * chunk // BLOCK, (i + 1) * chunk // BLOCK):
            before_ref[b] = total
            total = total + dot_tn(rows_of(k_ref, b), rows_of(v_ref, b))
    total_ref[...] = total
    last = [pltpu.make_async_copy(before_ref, before_hbm, out_sems.at[2])]
    last += [pltpu.make_async_copy(total_ref, out_hbm.at[i], out_sems.at[3 + i]) for i in range(NX)]
    for copy in last:
        copy.start()
    for copy in sent + last:
        copy.wait()


def row_kernel(states_ref, before_ref, total_ref):
    x = lax.axis_index("x")
    before = jnp.zeros((HD, HD), f32)
    total = jnp.zeros((HD, HD), f32)
    for i in range(NX):
        state = states_ref[i]
        total = total + state
        before = before + jnp.where(i < x, state, 0.0)
    before_ref[...] = before
    sent = total.astype(bf16)
    for i in range(NY):
        total_ref[i] = sent


def block_rows(q, keys, values, bias, upper):
    key_blocks = [dot_nt(q, key) for key in keys]
    near = key_blocks[-1]
    high, low = split_pair(jnp.where(upper, 0.0, near))
    linear = dot(high, values[-1]) + dot(low, values[-1])
    if bias is not None:
        key_blocks = [s if b is None else s + b for s, b in zip(key_blocks, bias)]
    scores = [jnp.where(upper, key_blocks[0], near)] + key_blocks[1:-1]
    top = scores[0]
    for s in scores[1:]:
        top = jnp.maximum(top, s)
    top = jnp.max(top, axis=-1, keepdims=True)
    weights = [jnp.exp2((s - top) * log2e_scale) for s in scores]
    ends = weights[0]
    parts = [jnp.where(upper, ends, 0.0)] + weights[1:] + [jnp.where(upper, 0.0, ends)]
    soft = None
    for part, value in zip(parts, values):
        term = dot(part.astype(bf16), value)
        soft = term if soft is None else soft + term
    return normalize(soft) * 0.5, linear


def upper_mask():
    rows = lax.broadcasted_iota(jnp.int32, (BLOCK, BLOCK), 0)
    cols = lax.broadcasted_iota(jnp.int32, (BLOCK, BLOCK), 1)
    return cols > rows


def prior_state(before_ref, totals_ref):
    y = lax.axis_index("y")
    prior = before_ref[...]
    for i in range(NY):
        prior = prior + jnp.where(i < y, totals_ref[i].astype(f32), 0.0)
    return prior


def mix(q, soft, linear, state):
    upper, lower = split_pair(state)
    both = dot(q, jnp.concatenate([upper, lower], axis=1))
    linear = linear + (both[:, :HD] + both[:, HD:])
    return (soft + normalize(linear) * 0.5).astype(bf16)


def inner_kernel(q_ref, k_ref, v_ref, within_ref, before_ref, totals_ref, out_ref):
    upper = upper_mask()
    prior = prior_state(before_ref, totals_ref)
    near = W // BLOCK
    for b in range(near, q_ref.shape[0] // BLOCK):
        q = rows_of(q_ref, b)
        keys = [rows_of(k_ref, b - near + j) for j in range(near + 1)]
        values = [rows_of(v_ref, b - near + j) for j in range(near + 1)]
        soft, linear = block_rows(q, keys, values, None, upper)
        out_ref[b - near] = mix(q, soft, linear, prior + within_ref[b])


def outer_kernel(
    q_ref, k_ref, v_ref, rim_hbm, within_ref, before_ref, totals_ref, inner_ref, out_hbm, rim_ref, out_ref, sems, out_sems
):
    near = W // BLOCK
    copies = []
    for j in reversed(range(near)):
        part = pl.ds(j * BLOCK, BLOCK)
        copies.append(pltpu.make_async_copy(rim_hbm.at[:, part], rim_ref.at[:, part], sems.at[j]))
        copies[-1].start()
    sent = [pltpu.make_async_copy(inner_ref, out_hbm.at[pl.ds(near, near)], out_sems.at[near])]
    sent[0].start()
    upper = upper_mask()
    prior = prior_state(before_ref, totals_ref)
    first = jnp.logical_and(lax.axis_index("y") == 0, lax.axis_index("x") == 0)
    hidden = jnp.where(first, far_below, 0.0).astype(f32)
    for b in reversed(range(near)):
        copies[near - 1 - b].wait()
        keys, values, bias = [], [], []
        for j in range(near + 1):
            at = b + j
            if at < near:
                keys.append(rim_ref[0, at * BLOCK : (at + 1) * BLOCK, :])
                values.append(rim_ref[1, at * BLOCK : (at + 1) * BLOCK, :])
                bias.append(hidden)
            else:
                keys.append(rows_of(k_ref, at - near))
                values.append(rows_of(v_ref, at - near))
                bias.append(None)
        q = rows_of(q_ref, b)
        soft, linear = block_rows(q, keys, values, bias, upper)
        out_ref[b] = mix(q, soft, linear, prior + within_ref[b])
        sent.append(pltpu.make_async_copy(out_ref.at[b], out_hbm.at[b], out_sems.at[b]))
        sent[-1].start()
    for copy in sent:
        copy.wait()


def unit_kernel(first_ref, second_ref, out_ref):
    half = first_ref.shape[0]
    odd = lax.axis_index("x") % 2 == 1
    first, second = first_ref[...], second_ref[...]
    out_ref[:half, :] = jnp.where(odd, second, first)
    out_ref[half:, :] = jnp.where(odd, first, second)


def project_kernel(mixed_ref, *refs):
    units, given_ref, kept_ref = refs[:-2], refs[-2], refs[-1]
    y, x, c = lax.axis_index("y"), lax.axis_index("x"), lax.axis_index("c")
    turn = way(x, c)
    given, kept = [], []
    for step in unit_steps:
        head = lax.rem(y + turn * step + NY, NY)
        given.append(mixed_ref[head, pl.ds(pl.multiple_of((1 - c) * HD, HD), HD), :])
        kept.append(mixed_ref[head, pl.ds(pl.multiple_of(c * HD, HD), HD), :])
    left = [
        jnp.concatenate(
            [jnp.concatenate(given[i : i + 2], axis=1), jnp.concatenate(kept[i : i + 2], axis=1)], axis=0
        )
        for i in range(0, NY, 2)
    ]
    width = 512
    for n in range(kept_ref.shape[1] // width):
        cols = slice(n * width, (n + 1) * width)
        total = None
        for i in range(0, NY, 2):
            rows = jnp.concatenate([units[i][:, cols], units[i + 1][:, cols]], axis=0)
            term = dot(left[i // 2], rows)
            total = term if total is None else total + term
        given_ref[:, cols] = total[:HD].astype(bf16)
        kept_ref[:, cols] = total[HD:]


def add_kernel(kept_ref, taken_ref, out_ref):
    out_ref[...] = (kept_ref[...] + taken_ref[...].astype(f32)).astype(bf16)


def linear_index(y, x, z, c):
    return ((y % NY * NX + x % NX) * NZ + z % NZ) * NC + c


def moved(shard, source):
    pairs = []
    for y in range(NY):
        for x in range(NX):
            for z in range(NZ):
                for c in range(NC):
                    at = source(y, x, z, c)
                    if at is not None:
                        pairs.append((linear_index(*at), linear_index(y, x, z, c)))
    return lax.ppermute(shard, AXES, pairs)


def first_chunk(y, x, z, c):
    if x // 2 == c:
        return (y, x ^ 1, z, 1 - c)
    return (y, 3 - x, z, c)


def second_chunk(y, x, z, c):
    return (y, x, z, 1 - c) if x // 2 == c else (y, x ^ 2, z, c)


unit_steps = (0, 1, 2, 3, 4, -1, -2, -3)


def way(x, c):
    return 1 - 2 * ((x + c) % 2)


def along(y, x, z, c):
    return (y + way(x, c), x, z, c)


def across(y, x, z, c):
    return (y, (x ^ 1) if c == 0 else ((x + 1) ^ 1) - 1, z, c)


def layer(queries, key_vectors, value_vectors, w_out):
    rows = queries.shape[0]
    wide = w_out.shape[1]

    def shape(dims, kind):
        return jax.ShapeDtypeStruct(dims, kind)

    chunk_a = moved(w_out, first_chunk)
    chunk_b = moved(w_out, second_chunk)
    states, within, rim = call(
        state_kernel,
        (shape((NX, HD, HD), f32), shape((rows // BLOCK, HD, HD), f32), shape((2, W, HD), bf16)),
        [ANY] * 2,
        grant=60 << 20, out_specs=[ANY] * 3,
        scratch=[pltpu.VMEM((rows, HD), bf16)] * 2
        + [pltpu.VMEM((rows // BLOCK, HD, HD), f32), pltpu.VMEM((HD, HD), f32)]
        + [pltpu.SemaphoreType.DMA((2, FETCHES)), pltpu.SemaphoreType.DMA((3 + NX,))],
    )(key_vectors, value_vectors)
    row_states = lax.all_to_all(states, "x", 0, 0, tiled=True)
    unit = call(unit_kernel, shape((2 * w_out.shape[0], wide), bf16), [VMEM] * 2)(chunk_b, chunk_a)
    y1 = moved(unit, along)
    rim = lax.ppermute(rim, ("y", "x"), [(i, i + 1) for i in range(NY * NX - 1)])
    before, totals = call(
        row_kernel, (shape((HD, HD), f32), shape((NY, HD, HD), bf16)), [VMEM]
    )(row_states)
    totals = lax.all_to_all(totals, "y", 0, 0, tiled=True)
    y2 = moved(y1, along)
    e1 = moved(y1, across)
    shared = (within, before, totals)
    inner = call(inner_kernel, shape((NZ // 2, rows // NZ, HD), bf16), [VMEM] * 6)(
        queries, key_vectors, value_vectors, *shared
    )
    y3 = moved(y2, along)
    e2 = moved(y2, across)
    mixed = call(
        outer_kernel, shape((NZ, rows // NZ, HD), bf16), [VMEM] * 3 + [ANY] + [VMEM] * 4,
        out_specs=ANY,
        scratch=[pltpu.VMEM((2, W, HD), bf16), pltpu.VMEM((W // BLOCK, BLOCK, HD), bf16)]
        + [pltpu.SemaphoreType.DMA((W // BLOCK,)), pltpu.SemaphoreType.DMA((1 + W // BLOCK,))],
    )(
        queries, key_vectors, value_vectors, rim, *shared, inner
    )
    mixed = lax.all_to_all(mixed, "z", 0, 0, tiled=True)
    y4 = moved(y3, along)
    e3 = moved(y3, across)
    given, kept = call(
        project_kernel, (shape((HD, wide), bf16), shape((HD, wide), f32)),
        [VMEM] * (1 + NY),
    )(mixed, unit, y1, y2, y3, y4, e1, e2, e3)
    taken = lax.ppermute(given, "c", [(0, 1), (1, 0)])
    return call(add_kernel, shape((HD, wide), bf16), [VMEM] * 2)(kept, taken)


def solution(mesh):
    fine = Mesh(mesh.devices.reshape(NY, NX, NZ, NC), AXES)
    split = P(("y", "x"), ("z", "c"))
    return jax.shard_map(
        layer,
        mesh=fine,
        in_specs=(split, split, split, P(("y", "x"), None)),
        out_specs=P(AXES, None),
        check_vma=False,
    )
```

```python
import math

import jax
import jax.numpy as jnp
from jax import lax
from jax.experimental import pallas as pl
from jax.experimental.pallas import tpu as pltpu
from jax.sharding import Mesh
from jax.sharding import PartitionSpec as P

HD = 128
W = 1024
BLOCK = 256
FETCHES = 4
NY, NX, NZ, NC = 8, 4, 8, 2
AXES = ("y", "x", "z", "c")

norm_eps = 1e-06
log2e_scale = math.log2(math.e) / math.sqrt(HD)
far_below = -1e30

f32, bf16 = jnp.float32, jnp.bfloat16


def dot(a, b):
    return lax.dot_general(a, b, (((1,), (0,)), ((), ())), preferred_element_type=f32)


def dot_nt(a, b):
    return lax.dot_general(a, b, (((1,), (1,)), ((), ())), preferred_element_type=f32)


def dot_tn(a, b):
    return lax.dot_general(a, b, (((0,), (0,)), ((), ())), preferred_element_type=f32)


def normalize(branch):
    return branch * lax.rsqrt(jnp.mean(branch * branch, axis=-1, keepdims=True) + norm_eps)


def split_pair(values):
    upper = values.astype(bf16)
    return upper, (values - upper.astype(f32)).astype(bf16)


VMEM = pl.BlockSpec(memory_space=pltpu.VMEM)
ANY = pl.BlockSpec(memory_space=pl.ANY)


def call(kernel, outs, in_specs, scratch=(), grant=12 << 20, out_specs=None):
    return pl.pallas_call(
        kernel,
        out_shape=outs,
        in_specs=in_specs,
        scratch_shapes=scratch,
        out_specs=out_specs or jax.tree.map(lambda _: VMEM, outs),
        compiler_params=pltpu.CompilerParams(vmem_limit_bytes=grant),
        cost_estimate=pl.CostEstimate(flops=1, transcendentals=0, bytes_accessed=64 << 20),
    )


def rows_of(ref, index):
    return ref[index * BLOCK : (index + 1) * BLOCK, :]


def state_kernel(k_hbm, v_hbm, out_hbm, before_hbm, rim_hbm, k_ref, v_ref, before_ref, total_ref, sems, out_sems):
    chunk = k_hbm.shape[0] // FETCHES
    copies = []
    for i in range(FETCHES):
        part = pl.ds(i * chunk, chunk)
        pair = (
            pltpu.make_async_copy(k_hbm.at[part], k_ref.at[part], sems.at[0, i]),
            pltpu.make_async_copy(v_hbm.at[part], v_ref.at[part], sems.at[1, i]),
        )
        for copy in pair:
            copy.start()
        copies.append(pair)
    tail = pl.ds(k_hbm.shape[0] - W, W)
    sent = [
        pltpu.make_async_copy(k_ref.at[tail], rim_hbm.at[0], out_sems.at[0]),
        pltpu.make_async_copy(v_ref.at[tail], rim_hbm.at[1], out_sems.at[1]),
    ]
    total = jnp.zeros((HD, HD), f32)
    for i in range(FETCHES):
        for copy in copies[i]:
            copy.wait()
        if i == FETCHES - 1:
            for copy in sent:
                copy.start()
        for b in range(i * chunk // BLOCK, (i + 1) * chunk // BLOCK):
            before_ref[b] = total
            total = total + dot_tn(rows_of(k_ref, b), rows_of(v_ref, b))
    total_ref[...] = total
    last = [pltpu.make_async_copy(before_ref, before_hbm, out_sems.at[2])]
    last += [pltpu.make_async_copy(total_ref, out_hbm.at[i], out_sems.at[3 + i]) for i in range(NX)]
    for copy in last:
        copy.start()
    for copy in sent + last:
        copy.wait()


def row_kernel(states_ref, before_ref, total_ref):
    x = lax.axis_index("x")
    before = jnp.zeros((HD, HD), f32)
    total = jnp.zeros((HD, HD), f32)
    for i in range(NX):
        state = states_ref[i]
        total = total + state
        before = before + jnp.where(i < x, state, 0.0)
    before_ref[...] = before
    sent = total.astype(bf16)
    for i in range(NY):
        total_ref[i] = sent


def block_rows(q, keys, values, bias, upper):
    key_blocks = [dot_nt(q, key) for key in keys]
    near = key_blocks[-1]
    high, low = split_pair(jnp.where(upper, 0.0, near))
    linear = dot(high, values[-1]) + dot(low, values[-1])
    if bias is not None:
        key_blocks = [s if b is None else s + b for s, b in zip(key_blocks, bias)]
    scores = [jnp.where(upper, key_blocks[0], near)] + key_blocks[1:-1]
    top = scores[0]
    for s in scores[1:]:
        top = jnp.maximum(top, s)
    top = jnp.max(top, axis=-1, keepdims=True)
    weights = [jnp.exp2((s - top) * log2e_scale) for s in scores]
    ends = weights[0]
    parts = [jnp.where(upper, ends, 0.0)] + weights[1:] + [jnp.where(upper, 0.0, ends)]
    soft = None
    for part, value in zip(parts, values):
        term = dot(part.astype(bf16), value)
        soft = term if soft is None else soft + term
    return normalize(soft) * 0.5, linear


def upper_mask():
    rows = lax.broadcasted_iota(jnp.int32, (BLOCK, BLOCK), 0)
    cols = lax.broadcasted_iota(jnp.int32, (BLOCK, BLOCK), 1)
    return cols > rows


def prior_state(before_ref, totals_ref):
    y = lax.axis_index("y")
    prior = before_ref[...]
    for i in range(NY):
        prior = prior + jnp.where(i < y, totals_ref[i].astype(f32), 0.0)
    return prior


def mix(q, soft, linear, state):
    upper, lower = split_pair(state)
    both = dot(q, jnp.concatenate([upper, lower], axis=1))
    linear = linear + (both[:, :HD] + both[:, HD:])
    return (soft + normalize(linear) * 0.5).astype(bf16)


def inner_kernel(q_ref, k_ref, v_ref, rim_hbm, within_ref, before_ref, totals_ref, out_ref, rim_ref, sem):
    fetch = pltpu.make_async_copy(rim_hbm, rim_ref, sem)
    fetch.start()
    upper = upper_mask()
    prior = prior_state(before_ref, totals_ref)
    near = W // BLOCK
    for b in range(near, q_ref.shape[0] // BLOCK):
        q = rows_of(q_ref, b)
        keys = [rows_of(k_ref, b - near + j) for j in range(near + 1)]
        values = [rows_of(v_ref, b - near + j) for j in range(near + 1)]
        soft, linear = block_rows(q, keys, values, None, upper)
        out_ref[b - near] = mix(q, soft, linear, prior + within_ref[b])
    fetch.wait()


def outer_kernel(
    q_ref, k_ref, v_ref, rim_ref, within_ref, before_ref, totals_ref, inner_ref, out_hbm, out_ref, out_sems
):
    near = W // BLOCK
    sent = [pltpu.make_async_copy(inner_ref, out_hbm.at[pl.ds(near, near)], out_sems.at[near])]
    sent[0].start()
    upper = upper_mask()
    prior = prior_state(before_ref, totals_ref)
    first = jnp.logical_and(lax.axis_index("y") == 0, lax.axis_index("x") == 0)
    hidden = jnp.where(first, far_below, 0.0).astype(f32)
    for b in reversed(range(near)):
        keys, values, bias = [], [], []
        for j in range(near + 1):
            at = b + j
            if at < near:
                keys.append(rim_ref[0, at * BLOCK : (at + 1) * BLOCK, :])
                values.append(rim_ref[1, at * BLOCK : (at + 1) * BLOCK, :])
                bias.append(hidden)
            else:
                keys.append(rows_of(k_ref, at - near))
                values.append(rows_of(v_ref, at - near))
                bias.append(None)
        q = rows_of(q_ref, b)
        soft, linear = block_rows(q, keys, values, bias, upper)
        out_ref[b] = mix(q, soft, linear, prior + within_ref[b])
        sent.append(pltpu.make_async_copy(out_ref.at[b], out_hbm.at[b], out_sems.at[b]))
        sent[-1].start()
    for copy in sent:
        copy.wait()


def unit_kernel(first_ref, second_ref, out_ref):
    half = first_ref.shape[0]
    odd = lax.axis_index("x") % 2 == 1
    first, second = first_ref[...], second_ref[...]
    out_ref[:half, :] = jnp.where(odd, second, first)
    out_ref[half:, :] = jnp.where(odd, first, second)


def project_kernel(mixed_ref, *refs):
    units, given_ref, kept_ref = refs[:-2], refs[-2], refs[-1]
    y, x, c = lax.axis_index("y"), lax.axis_index("x"), lax.axis_index("c")
    turn = way(x, c)
    given, kept = [], []
    for step in unit_steps:
        head = lax.rem(y + turn * step + NY, NY)
        given.append(mixed_ref[head, pl.ds(pl.multiple_of((1 - c) * HD, HD), HD), :])
        kept.append(mixed_ref[head, pl.ds(pl.multiple_of(c * HD, HD), HD), :])
    left = [
        jnp.concatenate(
            [jnp.concatenate(given[i : i + 2], axis=1), jnp.concatenate(kept[i : i + 2], axis=1)], axis=0
        )
        for i in range(0, NY, 2)
    ]
    width = 512
    for n in range(kept_ref.shape[1] // width):
        cols = slice(n * width, (n + 1) * width)
        total = None
        for i in range(0, NY, 2):
            rows = jnp.concatenate([units[i][:, cols], units[i + 1][:, cols]], axis=0)
            term = dot(left[i // 2], rows)
            total = term if total is None else total + term
        given_ref[:, cols] = total[:HD].astype(bf16)
        kept_ref[:, cols] = total[HD:]


def add_kernel(kept_ref, taken_ref, out_ref):
    out_ref[...] = (kept_ref[...] + taken_ref[...].astype(f32)).astype(bf16)


def linear_index(y, x, z, c):
    return ((y % NY * NX + x % NX) * NZ + z % NZ) * NC + c


def moved(shard, source):
    pairs = []
    for y in range(NY):
        for x in range(NX):
            for z in range(NZ):
                for c in range(NC):
                    at = source(y, x, z, c)
                    if at is not None:
                        pairs.append((linear_index(*at), linear_index(y, x, z, c)))
    return lax.ppermute(shard, AXES, pairs)


def first_chunk(y, x, z, c):
    if x // 2 == c:
        return (y, x ^ 1, z, 1 - c)
    return (y, 3 - x, z, c)


def second_chunk(y, x, z, c):
    return (y, x, z, 1 - c) if x // 2 == c else (y, x ^ 2, z, c)


unit_steps = (0, 1, 2, 3, 4, -1, -2, -3)


def way(x, c):
    return 1 - 2 * ((x + c) % 2)


def along(y, x, z, c):
    return (y + way(x, c), x, z, c)


def across(y, x, z, c):
    return (y, (x ^ 1) if c == 0 else ((x + 1) ^ 1) - 1, z, c)


def layer(queries, key_vectors, value_vectors, w_out):
    rows = queries.shape[0]
    wide = w_out.shape[1]

    def shape(dims, kind):
        return jax.ShapeDtypeStruct(dims, kind)

    chunk_a = moved(w_out, first_chunk)
    chunk_b = moved(w_out, second_chunk)
    states, within, rim = call(
        state_kernel,
        (shape((NX, HD, HD), f32), shape((rows // BLOCK, HD, HD), f32), shape((2, W, HD), bf16)),
        [ANY] * 2,
        grant=60 << 20, out_specs=[ANY] * 3,
        scratch=[pltpu.VMEM((rows, HD), bf16)] * 2
        + [pltpu.VMEM((rows // BLOCK, HD, HD), f32), pltpu.VMEM((HD, HD), f32)]
        + [pltpu.SemaphoreType.DMA((2, FETCHES)), pltpu.SemaphoreType.DMA((3 + NX,))],
    )(key_vectors, value_vectors)
    row_states = lax.all_to_all(states, "x", 0, 0, tiled=True)
    unit = call(unit_kernel, shape((2 * w_out.shape[0], wide), bf16), [VMEM] * 2)(chunk_b, chunk_a)
    y1 = moved(unit, along)
    rim = lax.ppermute(rim, ("y", "x"), [(i, i + 1) for i in range(NY * NX - 1)])
    before, totals = call(row_kernel, (shape((HD, HD), f32), shape((NY, HD, HD), bf16)), [VMEM])(row_states)
    totals = lax.all_to_all(totals, "y", 0, 0, tiled=True)
    y2 = moved(y1, along)
    e1 = moved(y1, across)
    shared = (within, before, totals)
    inner, rim = call(
        inner_kernel, (shape((NZ // 2, rows // NZ, HD), bf16), shape(rim.shape, bf16)),
        [VMEM] * 3 + [ANY] + [VMEM] * 3, scratch=[pltpu.SemaphoreType.DMA],
    )(
        queries, key_vectors, value_vectors, rim, *shared
    )
    y3 = moved(y2, along)
    e2 = moved(y2, across)
    mixed = call(
        outer_kernel, shape((NZ, rows // NZ, HD), bf16), [VMEM] * 8, out_specs=ANY,
        scratch=[pltpu.VMEM((W // BLOCK, BLOCK, HD), bf16), pltpu.SemaphoreType.DMA((1 + W // BLOCK,))],
    )(
        queries, key_vectors, value_vectors, rim, *shared, inner
    )
    mixed = lax.all_to_all(mixed, "z", 0, 0, tiled=True)
    y4 = moved(y3, along)
    e3 = moved(y3, across)
    given, kept = call(
        project_kernel, (shape((HD, wide), bf16), shape((HD, wide), f32)),
        [VMEM] * (1 + NY),
    )(mixed, unit, y1, y2, y3, y4, e1, e2, e3)
    taken = lax.ppermute(given, "c", [(0, 1), (1, 0)])
    return call(add_kernel, shape((HD, wide), bf16), [VMEM] * 2)(kept, taken)


def solution(mesh):
    fine = Mesh(mesh.devices.reshape(NY, NX, NZ, NC), AXES)
    split = P(("y", "x"), ("z", "c"))
    return jax.shard_map(
        layer,
        mesh=fine,
        in_specs=(split, split, split, P(("y", "x"), None)),
        out_specs=P(AXES, None),
        check_vma=False,
    )
```

```python
import math

import jax
import jax.numpy as jnp
from jax import lax
from jax.experimental import pallas as pl
from jax.experimental.pallas import tpu as pltpu
from jax.sharding import Mesh
from jax.sharding import PartitionSpec as P

HD = 128
W = 1024
BLOCK = 256
FETCHES = 4
NY, NX, NZ, NC = 8, 4, 8, 2
AXES = ("y", "x", "z", "c")

norm_eps = 1e-06
log2e_scale = math.log2(math.e) / math.sqrt(HD)
far_below = -1e30

f32, bf16 = jnp.float32, jnp.bfloat16


def dot(a, b):
    return lax.dot_general(a, b, (((1,), (0,)), ((), ())), preferred_element_type=f32)


def dot_nt(a, b):
    return lax.dot_general(a, b, (((1,), (1,)), ((), ())), preferred_element_type=f32)


def dot_tn(a, b):
    return lax.dot_general(a, b, (((0,), (0,)), ((), ())), preferred_element_type=f32)


def normalize(branch):
    return branch * lax.rsqrt(jnp.mean(branch * branch, axis=-1, keepdims=True) + norm_eps)


def split_pair(values):
    upper = values.astype(bf16)
    return upper, (values - upper.astype(f32)).astype(bf16)


VMEM = pl.BlockSpec(memory_space=pltpu.VMEM)
ANY = pl.BlockSpec(memory_space=pl.ANY)


def call(kernel, outs, in_specs, scratch=(), grant=12 << 20, out_specs=None):
    return pl.pallas_call(
        kernel,
        out_shape=outs,
        in_specs=in_specs,
        scratch_shapes=scratch,
        out_specs=out_specs or jax.tree.map(lambda _: VMEM, outs),
        compiler_params=pltpu.CompilerParams(vmem_limit_bytes=grant),
        cost_estimate=pl.CostEstimate(flops=1, transcendentals=0, bytes_accessed=64 << 20),
    )


def rows_of(ref, index):
    return ref[index * BLOCK : (index + 1) * BLOCK, :]


def state_kernel(k_hbm, v_hbm, out_hbm, before_hbm, rim_hbm, k_ref, v_ref, before_ref, total_ref, sems, out_sems):
    chunk = k_hbm.shape[0] // FETCHES
    copies = []
    for i in range(FETCHES):
        part = pl.ds(i * chunk, chunk)
        pair = (
            pltpu.make_async_copy(k_hbm.at[part], k_ref.at[part], sems.at[0, i]),
            pltpu.make_async_copy(v_hbm.at[part], v_ref.at[part], sems.at[1, i]),
        )
        for copy in pair:
            copy.start()
        copies.append(pair)
    tail = pl.ds(k_hbm.shape[0] - W, W)
    sent = [
        pltpu.make_async_copy(k_ref.at[tail], rim_hbm.at[0], out_sems.at[0]),
        pltpu.make_async_copy(v_ref.at[tail], rim_hbm.at[1], out_sems.at[1]),
    ]
    total = jnp.zeros((HD, HD), f32)
    for i in range(FETCHES):
        for copy in copies[i]:
            copy.wait()
        if i == FETCHES - 1:
            for copy in sent:
                copy.start()
        for b in range(i * chunk // BLOCK, (i + 1) * chunk // BLOCK):
            before_ref[b] = total
            total = total + dot_tn(rows_of(k_ref, b), rows_of(v_ref, b))
    total_ref[...] = total
    last = [pltpu.make_async_copy(before_ref, before_hbm, out_sems.at[2])]
    last += [pltpu.make_async_copy(total_ref, out_hbm.at[i], out_sems.at[3 + i]) for i in range(NX)]
    for copy in last:
        copy.start()
    for copy in sent + last:
        copy.wait()


def row_kernel(states_ref, before_ref, total_ref):
    x = lax.axis_index("x")
    before = jnp.zeros((HD, HD), f32)
    total = jnp.zeros((HD, HD), f32)
    for i in range(NX):
        state = states_ref[i]
        total = total + state
        before = before + jnp.where(i < x, state, 0.0)
    before_ref[...] = before
    sent = total.astype(bf16)
    for i in range(NY):
        total_ref[i] = sent


def block_rows(q, keys, values, bias, upper):
    key_blocks = [dot_nt(q, key) for key in keys]
    near = key_blocks[-1]
    high, low = split_pair(jnp.where(upper, 0.0, near))
    linear = dot(high, values[-1]) + dot(low, values[-1])
    if bias is not None:
        key_blocks = [s if b is None else s + b for s, b in zip(key_blocks, bias)]
    scores = [jnp.where(upper, key_blocks[0], near)] + key_blocks[1:-1]
    top = scores[0]
    for s in scores[1:]:
        top = jnp.maximum(top, s)
    top = jnp.max(top, axis=-1, keepdims=True)
    weights = [jnp.exp2((s - top) * log2e_scale) for s in scores]
    ends = weights[0]
    parts = [jnp.where(upper, ends, 0.0)] + weights[1:] + [jnp.where(upper, 0.0, ends)]
    soft = None
    for part, value in zip(parts, values):
        term = dot(part.astype(bf16), value)
        soft = term if soft is None else soft + term
    return normalize(soft) * 0.5, linear


def upper_mask():
    rows = lax.broadcasted_iota(jnp.int32, (BLOCK, BLOCK), 0)
    cols = lax.broadcasted_iota(jnp.int32, (BLOCK, BLOCK), 1)
    return cols > rows


def prior_state(before_ref, totals_ref):
    y = lax.axis_index("y")
    prior = before_ref[...]
    for i in range(NY):
        prior = prior + jnp.where(i < y, totals_ref[i].astype(f32), 0.0)
    return prior


def mix(q, soft, linear, state):
    upper, lower = split_pair(state)
    both = dot(q, jnp.concatenate([upper, lower], axis=1))
    linear = linear + (both[:, :HD] + both[:, HD:])
    return (soft + normalize(linear) * 0.5).astype(bf16)


def inner_kernel(q_ref, k_ref, v_ref, out_hbm, held_ref, sems):
    sent = []
    upper = upper_mask()
    near = W // BLOCK
    for b in range(q_ref.shape[0] // BLOCK - near):
        q = rows_of(q_ref, near + b)
        keys = [rows_of(k_ref, b + j) for j in range(near + 1)]
        values = [rows_of(v_ref, b + j) for j in range(near + 1)]
        soft, linear = block_rows(q, keys, values, None, upper)
        held_ref[b, 0] = soft
        held_ref[b, 1] = linear
        sent.append(pltpu.make_async_copy(held_ref.at[b], out_hbm.at[b], sems.at[b]))
        sent[-1].start()
    for copy in sent:
        copy.wait()


def outer_kernel(
    q_ref, k_ref, v_ref, rim_hbm, within_hbm, inner_hbm, before_ref, totals_ref,
    out_hbm, rim_ref, within_ref, inner_ref, out_ref, sems, out_sems,
):
    near = W // BLOCK
    fetches = [
        pltpu.make_async_copy(source, target, sems.at[i])
        for i, (source, target) in enumerate(
            ((within_hbm, within_ref), (inner_hbm, inner_ref), (rim_hbm, rim_ref))
        )
    ]
    for fetch in fetches:
        fetch.start()
    sent = []

    def send(b):
        sent.append(pltpu.make_async_copy(out_ref.at[b], out_hbm.at[b], out_sems.at[b]))
        sent[-1].start()

    upper = upper_mask()
    prior = prior_state(before_ref, totals_ref)
    fetches[0].wait()
    fetches[1].wait()
    for b in range(near, q_ref.shape[0] // BLOCK):
        soft, linear = inner_ref[b - near, 0], inner_ref[b - near, 1]
        out_ref[b] = mix(rows_of(q_ref, b), soft, linear, prior + within_ref[b])
        send(b)
    fetches[2].wait()
    first = jnp.logical_and(lax.axis_index("y") == 0, lax.axis_index("x") == 0)
    hidden = jnp.where(first, far_below, 0.0).astype(f32)
    for b in range(near):
        keys, values, bias = [], [], []
        for j in range(near + 1):
            at = b + j
            if at < near:
                keys.append(rim_ref[0, at * BLOCK : (at + 1) * BLOCK, :])
                values.append(rim_ref[1, at * BLOCK : (at + 1) * BLOCK, :])
                bias.append(hidden)
            else:
                keys.append(rows_of(k_ref, at - near))
                values.append(rows_of(v_ref, at - near))
                bias.append(None)
        q = rows_of(q_ref, b)
        soft, linear = block_rows(q, keys, values, bias, upper)
        out_ref[b] = mix(q, soft, linear, prior + within_ref[b])
        send(b)
    for copy in sent:
        copy.wait()


def unit_kernel(first_ref, second_ref, out_ref):
    half = first_ref.shape[0]
    odd = lax.axis_index("x") % 2 == 1
    first, second = first_ref[...], second_ref[...]
    out_ref[:half, :] = jnp.where(odd, second, first)
    out_ref[half:, :] = jnp.where(odd, first, second)


def project_kernel(mixed_ref, *refs):
    units, given_ref, kept_ref = refs[:-2], refs[-2], refs[-1]
    y, x, c = lax.axis_index("y"), lax.axis_index("x"), lax.axis_index("c")
    turn = way(x, c)
    given, kept = [], []
    for step in unit_steps:
        head = lax.rem(y + turn * step + NY, NY)
        given.append(mixed_ref[head, pl.ds(pl.multiple_of((1 - c) * HD, HD), HD), :])
        kept.append(mixed_ref[head, pl.ds(pl.multiple_of(c * HD, HD), HD), :])
    left = [
        jnp.concatenate(
            [jnp.concatenate(given[i : i + 2], axis=1), jnp.concatenate(kept[i : i + 2], axis=1)], axis=0
        )
        for i in range(0, NY, 2)
    ]
    width = 512
    for n in range(kept_ref.shape[1] // width):
        cols = slice(n * width, (n + 1) * width)
        total = None
        for i in range(0, NY, 2):
            rows = jnp.concatenate([units[i][:, cols], units[i + 1][:, cols]], axis=0)
            term = dot(left[i // 2], rows)
            total = term if total is None else total + term
        given_ref[:, cols] = total[:HD].astype(bf16)
        kept_ref[:, cols] = total[HD:]


def add_kernel(kept_ref, taken_ref, out_ref):
    out_ref[...] = (kept_ref[...] + taken_ref[...].astype(f32)).astype(bf16)


def linear_index(y, x, z, c):
    return ((y % NY * NX + x % NX) * NZ + z % NZ) * NC + c


def moved(shard, source):
    pairs = []
    for y in range(NY):
        for x in range(NX):
            for z in range(NZ):
                for c in range(NC):
                    at = source(y, x, z, c)
                    if at is not None:
                        pairs.append((linear_index(*at), linear_index(y, x, z, c)))
    return lax.ppermute(shard, AXES, pairs)


def first_chunk(y, x, z, c):
    if x // 2 == c:
        return (y, x ^ 1, z, 1 - c)
    return (y, 3 - x, z, c)


def second_chunk(y, x, z, c):
    return (y, x, z, 1 - c) if x // 2 == c else (y, x ^ 2, z, c)


unit_steps = (0, 1, 2, 3, 4, -1, -2, -3)


def way(x, c):
    return 1 - 2 * ((x + c) % 2)


def along(y, x, z, c):
    return (y + way(x, c), x, z, c)


def across(y, x, z, c):
    return (y, (x ^ 1) if c == 0 else ((x + 1) ^ 1) - 1, z, c)


def layer(queries, key_vectors, value_vectors, w_out):
    rows = queries.shape[0]
    wide = w_out.shape[1]

    def shape(dims, kind):
        return jax.ShapeDtypeStruct(dims, kind)

    chunk_a = moved(w_out, first_chunk)
    chunk_b = moved(w_out, second_chunk)
    states, within, rim = call(
        state_kernel,
        (shape((NX, HD, HD), f32), shape((rows // BLOCK, HD, HD), f32), shape((2, W, HD), bf16)),
        [ANY] * 2,
        grant=60 << 20, out_specs=[ANY] * 3,
        scratch=[pltpu.VMEM((rows, HD), bf16)] * 2
        + [pltpu.VMEM((rows // BLOCK, HD, HD), f32), pltpu.VMEM((HD, HD), f32)]
        + [pltpu.SemaphoreType.DMA((2, FETCHES)), pltpu.SemaphoreType.DMA((3 + NX,))],
    )(key_vectors, value_vectors)
    row_states = lax.all_to_all(states, "x", 0, 0, tiled=True)
    unit = call(unit_kernel, shape((2 * w_out.shape[0], wide), bf16), [VMEM] * 2)(chunk_b, chunk_a)
    y1 = moved(unit, along)
    rim = lax.ppermute(rim, ("y", "x"), [(i, i + 1) for i in range(NY * NX - 1)])
    before, totals = call(
        row_kernel, (shape((HD, HD), f32), shape((NY, HD, HD), bf16)), [VMEM]
    )(row_states)
    totals = lax.all_to_all(totals, "y", 0, 0, tiled=True)
    y2 = moved(y1, along)
    e1 = moved(y1, across)
    half = (W // BLOCK, 2, BLOCK, HD)
    inner = call(
        inner_kernel, shape(half, f32), [VMEM] * 3, out_specs=ANY,
        scratch=[pltpu.VMEM(half, f32), pltpu.SemaphoreType.DMA((W // BLOCK,))],
    )(queries, key_vectors, value_vectors)
    y3 = moved(y2, along)
    e2 = moved(y2, across)
    mixed_shape = (NZ, rows // NZ, HD)
    mixed = call(
        outer_kernel, shape(mixed_shape, bf16), [VMEM] * 3 + [ANY] * 3 + [VMEM] * 2,
        out_specs=ANY,
        scratch=[pltpu.VMEM((2, W, HD), bf16), pltpu.VMEM((rows // BLOCK, HD, HD), f32)]
        + [pltpu.VMEM(half, f32), pltpu.VMEM(mixed_shape, bf16)]
        + [pltpu.SemaphoreType.DMA((3,)), pltpu.SemaphoreType.DMA((NZ,))],
    )(queries, key_vectors, value_vectors, rim, within, inner, before, totals)
    mixed = lax.all_to_all(mixed, "z", 0, 0, tiled=True)
    y4 = moved(y3, along)
    e3 = moved(y3, across)
    given, kept = call(
        project_kernel, (shape((HD, wide), bf16), shape((HD, wide), f32)),
        [VMEM] * (1 + NY),
    )(mixed, unit, y1, y2, y3, y4, e1, e2, e3)
    taken = lax.ppermute(given, "c", [(0, 1), (1, 0)])
    return call(add_kernel, shape((HD, wide), bf16), [VMEM] * 2)(kept, taken)


def solution(mesh):
    fine = Mesh(mesh.devices.reshape(NY, NX, NZ, NC), AXES)
    split = P(("y", "x"), ("z", "c"))
    return jax.shard_map(
        layer,
        mesh=fine,
        in_specs=(split, split, split, P(("y", "x"), None)),
        out_specs=P(AXES, None),
        check_vma=False,
    )
```

```python
import math

import jax
import jax.numpy as jnp
from jax import lax
from jax.experimental import pallas as pl
from jax.experimental.pallas import tpu as pltpu
from jax.sharding import Mesh
from jax.sharding import PartitionSpec as P

HD = 128
W = 1024
BLOCK = 256
FETCHES = 4
NY, NX, NZ, NC = 8, 4, 8, 2
AXES = ("y", "x", "z", "c")

norm_eps = 1e-06
log2e_scale = math.log2(math.e) / math.sqrt(HD)
far_below = -1e30

f32, bf16 = jnp.float32, jnp.bfloat16


def dot(a, b):
    return lax.dot_general(a, b, (((1,), (0,)), ((), ())), preferred_element_type=f32)


def dot_nt(a, b):
    return lax.dot_general(a, b, (((1,), (1,)), ((), ())), preferred_element_type=f32)


def dot_tn(a, b):
    return lax.dot_general(a, b, (((0,), (0,)), ((), ())), preferred_element_type=f32)


def normalize(branch):
    return branch * lax.rsqrt(jnp.mean(branch * branch, axis=-1, keepdims=True) + norm_eps)


def split_pair(values):
    upper = values.astype(bf16)
    return upper, (values - upper.astype(f32)).astype(bf16)


VMEM = pl.BlockSpec(memory_space=pltpu.VMEM)
ANY = pl.BlockSpec(memory_space=pl.ANY)


def call(kernel, outs, in_specs, nbytes=64 << 20, scratch=(), grant=12 << 20, out_specs=None):
    return pl.pallas_call(
        kernel,
        out_shape=outs,
        in_specs=in_specs,
        scratch_shapes=scratch,
        out_specs=out_specs or jax.tree.map(lambda _: VMEM, outs),
        compiler_params=pltpu.CompilerParams(vmem_limit_bytes=grant),
        cost_estimate=pl.CostEstimate(flops=1, transcendentals=0, bytes_accessed=nbytes),
    )


def rows_of(ref, index):
    return ref[index * BLOCK : (index + 1) * BLOCK, :]


def state_kernel(k_hbm, v_hbm, out_hbm, before_hbm, rim_hbm, k_ref, v_ref, before_ref, total_ref, sems, out_sems):
    chunk = k_hbm.shape[0] // FETCHES
    copies = []
    for i in range(FETCHES):
        part = pl.ds(i * chunk, chunk)
        pair = (
            pltpu.make_async_copy(k_hbm.at[part], k_ref.at[part], sems.at[0, i]),
            pltpu.make_async_copy(v_hbm.at[part], v_ref.at[part], sems.at[1, i]),
        )
        for copy in pair:
            copy.start()
        copies.append(pair)
    tail = pl.ds(k_hbm.shape[0] - W, W)
    sent = [
        pltpu.make_async_copy(k_ref.at[tail], rim_hbm.at[0], out_sems.at[0]),
        pltpu.make_async_copy(v_ref.at[tail], rim_hbm.at[1], out_sems.at[1]),
    ]
    total = jnp.zeros((HD, HD), f32)
    for i in range(FETCHES):
        for copy in copies[i]:
            copy.wait()
        if i == FETCHES - 1:
            for copy in sent:
                copy.start()
        for b in range(i * chunk // BLOCK, (i + 1) * chunk // BLOCK):
            before_ref[b] = total
            total = total + dot_tn(rows_of(k_ref, b), rows_of(v_ref, b))
    total_ref[...] = total
    last = [pltpu.make_async_copy(before_ref, before_hbm, out_sems.at[2])]
    last += [pltpu.make_async_copy(total_ref, out_hbm.at[i], out_sems.at[3 + i]) for i in range(NX)]
    for copy in last:
        copy.start()
    for copy in sent + last:
        copy.wait()


def row_kernel(states_ref, before_ref, total_ref):
    x = lax.axis_index("x")
    before = jnp.zeros((HD, HD), f32)
    total = jnp.zeros((HD, HD), f32)
    for i in range(NX):
        state = states_ref[i]
        total = total + state
        before = before + jnp.where(i < x, state, 0.0)
    before_ref[...] = before
    sent = total.astype(bf16)
    for i in range(NY):
        total_ref[i] = sent


def block_rows(q, keys, values, bias, upper):
    key_blocks = [dot_nt(q, key) for key in keys]
    near = key_blocks[-1]
    high, low = split_pair(jnp.where(upper, 0.0, near))
    linear = dot(high, values[-1]) + dot(low, values[-1])
    if bias is not None:
        key_blocks = [s if b is None else s + b for s, b in zip(key_blocks, bias)]
    scores = [jnp.where(upper, key_blocks[0], near)] + key_blocks[1:-1]
    top = scores[0]
    for s in scores[1:]:
        top = jnp.maximum(top, s)
    top = jnp.max(top, axis=-1, keepdims=True)
    weights = [jnp.exp2((s - top) * log2e_scale) for s in scores]
    ends = weights[0]
    parts = [jnp.where(upper, ends, 0.0)] + weights[1:] + [jnp.where(upper, 0.0, ends)]
    soft = None
    for part, value in zip(parts, values):
        term = dot(part.astype(bf16), value)
        soft = term if soft is None else soft + term
    return normalize(soft) * 0.5, linear


def upper_mask():
    rows = lax.broadcasted_iota(jnp.int32, (BLOCK, BLOCK), 0)
    cols = lax.broadcasted_iota(jnp.int32, (BLOCK, BLOCK), 1)
    return cols > rows


def prior_state(before_ref, totals_ref):
    y = lax.axis_index("y")
    prior = before_ref[...]
    for i in range(NY):
        prior = prior + jnp.where(i < y, totals_ref[i].astype(f32), 0.0)
    return prior


def mix(q, soft, linear, state):
    upper, lower = split_pair(state)
    both = dot(q, jnp.concatenate([upper, lower], axis=1))
    linear = linear + (both[:, :HD] + both[:, HD:])
    return (soft + normalize(linear) * 0.5).astype(bf16)


def inner_kernel(q_ref, k_ref, v_ref, rim_hbm, within_ref, before_ref, totals_ref, out_ref, rim_ref, sem):
    fetch = pltpu.make_async_copy(rim_hbm, rim_ref, sem)
    fetch.start()
    upper = upper_mask()
    prior = prior_state(before_ref, totals_ref)
    near = W // BLOCK
    for b in range(near, q_ref.shape[0] // BLOCK):
        q = rows_of(q_ref, b)
        keys = [rows_of(k_ref, b - near + j) for j in range(near + 1)]
        values = [rows_of(v_ref, b - near + j) for j in range(near + 1)]
        soft, linear = block_rows(q, keys, values, None, upper)
        out_ref[b - near] = mix(q, soft, linear, prior + within_ref[b])
    fetch.wait()


def outer_kernel(
    q_ref, k_ref, v_ref, rim_ref, within_ref, before_ref, totals_ref, inner_ref, out_hbm, out_ref, out_sems
):
    near = W // BLOCK
    sent = [pltpu.make_async_copy(inner_ref, out_hbm.at[pl.ds(near, near)], out_sems.at[near])]
    sent[0].start()
    upper = upper_mask()
    prior = prior_state(before_ref, totals_ref)
    first = jnp.logical_and(lax.axis_index("y") == 0, lax.axis_index("x") == 0)
    hidden = jnp.where(first, far_below, 0.0).astype(f32)
    for b in reversed(range(near)):
        keys, values, bias = [], [], []
        for j in range(near + 1):
            at = b + j
            if at < near:
                keys.append(rim_ref[0, at * BLOCK : (at + 1) * BLOCK, :])
                values.append(rim_ref[1, at * BLOCK : (at + 1) * BLOCK, :])
                bias.append(hidden)
            else:
                keys.append(rows_of(k_ref, at - near))
                values.append(rows_of(v_ref, at - near))
                bias.append(None)
        q = rows_of(q_ref, b)
        soft, linear = block_rows(q, keys, values, bias, upper)
        out_ref[b] = mix(q, soft, linear, prior + within_ref[b])
        sent.append(pltpu.make_async_copy(out_ref.at[b], out_hbm.at[b], out_sems.at[b]))
        sent[-1].start()
    for copy in sent:
        copy.wait()


def unit_kernel(first_ref, second_ref, out_ref):
    half = first_ref.shape[0]
    odd = lax.axis_index("x") % 2 == 1
    first, second = first_ref[...], second_ref[...]
    out_ref[:half, :] = jnp.where(odd, second, first)
    out_ref[half:, :] = jnp.where(odd, first, second)


def heads_of(mixed_ref, steps):
    y, x, c = lax.axis_index("y"), lax.axis_index("x"), lax.axis_index("c")
    turn = way(x, c)
    given, kept = [], []
    for step in steps:
        head = lax.rem(y + turn * step + NY, NY)
        given.append(mixed_ref[head, pl.ds(pl.multiple_of((1 - c) * HD, HD), HD), :])
        kept.append(mixed_ref[head, pl.ds(pl.multiple_of(c * HD, HD), HD), :])
    return [
        jnp.concatenate(
            [jnp.concatenate(given[i : i + 2], axis=1), jnp.concatenate(kept[i : i + 2], axis=1)], axis=0
        )
        for i in range(0, len(steps), 2)
    ]


def units_sum(left, units, cols):
    total = None
    for i in range(0, len(units), 2):
        rows = jnp.concatenate([units[i][:, cols], units[i + 1][:, cols]], axis=0)
        term = dot(left[i // 2], rows)
        total = term if total is None else total + term
    return total


def blocks_of_columns(ref, width=512):
    return [slice(n, n + width) for n in range(0, ref.shape[1], width)]


def early_kernel(mixed_ref, *refs):
    units, out_ref = refs[:-1], refs[-1]
    left = heads_of(mixed_ref, early_steps)
    for cols in blocks_of_columns(out_ref):
        out_ref[:, cols] = units_sum(left, units, cols)


def late_kernel(mixed_ref, early_ref, *refs):
    units, given_ref, kept_ref = refs[:-2], refs[-2], refs[-1]
    left = heads_of(mixed_ref, late_steps)
    for cols in blocks_of_columns(kept_ref):
        total = early_ref[:, cols] + units_sum(left, units, cols)
        given_ref[:, cols] = total[:HD].astype(bf16)
        kept_ref[:, cols] = total[HD:]


def add_kernel(kept_ref, taken_ref, out_ref):
    out_ref[...] = (kept_ref[...] + taken_ref[...].astype(f32)).astype(bf16)


def linear_index(y, x, z, c):
    return ((y % NY * NX + x % NX) * NZ + z % NZ) * NC + c


def moved(shard, source):
    pairs = []
    for y in range(NY):
        for x in range(NX):
            for z in range(NZ):
                for c in range(NC):
                    at = source(y, x, z, c)
                    if at is not None:
                        pairs.append((linear_index(*at), linear_index(y, x, z, c)))
    return lax.ppermute(shard, AXES, pairs)


def first_chunk(y, x, z, c):
    if x // 2 == c:
        return (y, x ^ 1, z, 1 - c)
    return (y, 3 - x, z, c)


def second_chunk(y, x, z, c):
    return (y, x, z, 1 - c) if x // 2 == c else (y, x ^ 2, z, c)


early_steps = (0, 1, 2, 3, -1, -2)
late_steps = (4, -3)


def way(x, c):
    return 1 - 2 * ((x + c) % 2)


def along(y, x, z, c):
    return (y + way(x, c), x, z, c)


def across(y, x, z, c):
    return (y, (x ^ 1) if c == 0 else ((x + 1) ^ 1) - 1, z, c)


def layer(queries, key_vectors, value_vectors, w_out):
    rows = queries.shape[0]
    wide = w_out.shape[1]

    def shape(dims, kind):
        return jax.ShapeDtypeStruct(dims, kind)

    chunk_a = moved(w_out, first_chunk)
    chunk_b = moved(w_out, second_chunk)
    states, within, rim = call(
        state_kernel,
        (shape((NX, HD, HD), f32), shape((rows // BLOCK, HD, HD), f32), shape((2, W, HD), bf16)),
        [ANY] * 2,
        grant=60 << 20, out_specs=[ANY] * 3,
        scratch=[pltpu.VMEM((rows, HD), bf16)] * 2
        + [pltpu.VMEM((rows // BLOCK, HD, HD), f32), pltpu.VMEM((HD, HD), f32)]
        + [pltpu.SemaphoreType.DMA((2, FETCHES)), pltpu.SemaphoreType.DMA((3 + NX,))],
    )(key_vectors, value_vectors)
    row_states = lax.all_to_all(states, "x", 0, 0, tiled=True)
    unit = call(unit_kernel, shape((2 * w_out.shape[0], wide), bf16), [VMEM] * 2)(chunk_b, chunk_a)
    y1 = moved(unit, along)
    rim = lax.ppermute(rim, ("y", "x"), [(i, i + 1) for i in range(NY * NX - 1)])
    before, totals = call(row_kernel, (shape((HD, HD), f32), shape((NY, HD, HD), bf16)), [VMEM], nbytes=0)(row_states)
    totals = lax.all_to_all(totals, "y", 0, 0, tiled=True)
    y2 = moved(y1, along)
    e1 = moved(y1, across)
    shared = (within, before, totals)
    inner, rim = call(
        inner_kernel, (shape((NZ // 2, rows // NZ, HD), bf16), shape(rim.shape, bf16)),
        [VMEM] * 3 + [ANY] + [VMEM] * 3, scratch=[pltpu.SemaphoreType.DMA],
    )(
        queries, key_vectors, value_vectors, rim, *shared
    )
    y3 = moved(y2, along)
    e2 = moved(y2, across)
    mixed = call(
        outer_kernel, shape((NZ, rows // NZ, HD), bf16), [VMEM] * 8, out_specs=ANY,
        scratch=[pltpu.VMEM((W // BLOCK, BLOCK, HD), bf16), pltpu.SemaphoreType.DMA((1 + W // BLOCK,))],
    )(
        queries, key_vectors, value_vectors, rim, *shared, inner
    )
    mixed = lax.all_to_all(mixed, "z", 0, 0, tiled=True)
    y4 = moved(y3, along)
    e3 = moved(y3, across)
    early = call(early_kernel, shape((2 * HD, wide), f32), [VMEM] * 7)(mixed, unit, y1, y2, y3, e1, e2)
    given, kept = call(late_kernel, (shape((HD, wide), bf16), shape((HD, wide), f32)), [VMEM] * 4)(mixed, early, y4, e3)
    taken = lax.ppermute(given, "c", [(0, 1), (1, 0)])
    return call(add_kernel, shape((HD, wide), bf16), [VMEM] * 2)(kept, taken)


def solution(mesh):
    fine = Mesh(mesh.devices.reshape(NY, NX, NZ, NC), AXES)
    split = P(("y", "x"), ("z", "c"))
    return jax.shard_map(
        layer,
        mesh=fine,
        in_specs=(split, split, split, P(("y", "x"), None)),
        out_specs=P(AXES, None),
        check_vma=False,
    )
```
